32 devices in a mesh: occ: 8 (over y, x, core), ao: 4 (over z).
Axes of the slice: x: 2, y: 2, z: 4, core: 2. Of those that a mesh axis runs over, the one named last changes fastest.
Arguments:
- coef: bfloat16 [2048, 8], P('ao', 'occ'), may hold values from -0.5 to 0.5
- half_ints: bfloat16 [8, 1024, 2048], P('occ', None, 'ao'), may hold values from -0.5 to 0.5
- metric_inv: bfloat16 [64, 128, 128], replicated, may hold values from -1 to 2, as said below
- dom_blocks: int32 [8, 8], P('occ'), may hold values from 0 to 63, as said below
- dom_len: int32 [8], P('occ'), may hold values from 2 to 8
Outputs:
- exchange_k: float32 [2048, 2048], P('ao', 'occ')
- fit_density: float32 [8192], replicated
The draws below stay inside these ranges and needn't reach their ends.
Inputs may be any that keep to these rules, and one draw needn't show every extreme that they name: `dom_blocks`: each row holds 8 different block numbers. `metric_inv`: full rank blocks.
All inputs are finite; a program needn't handle non-finite values.
Results may differ from the reference program's by a relative error of at most 0.0055.
Values may be sent and summed in bfloat16 or wider, within the bound.
No kernel may reach another device: no remote copies, remote signals or barrier semaphores. Data moves between devices by JAX's collectives and lax.ppermute only.
A program may use at most 128 MiB of HBM per device.

```python
import math
import jax
import jax.numpy as jnp
from jax import lax

BLK = 128
DOMB = 8
NFITB = 64
DOM = 1024
NAO = 2048
NOCC = 8
NFIT = 8192


def draw_metric_inv(key, part):
    noise = jax.random.normal(key, (NFITB, BLK, BLK), jnp.float32)
    return (jnp.eye(BLK, dtype=jnp.float32)[None] + 0.6 * noise / math.sqrt(BLK)).astype(jnp.bfloat16)


def draw_dom_blocks(key, part):
    scores = jax.random.randint(jax.random.fold_in(key, 7), (NOCC, NFITB), 0, 1 << 20)
    scores = scores * NFITB + jnp.arange(NFITB, dtype=jnp.int32)[None, :]
    order = jnp.argsort(scores, axis=1, stable=True)
    return order[:, :DOMB].astype(jnp.int32)


def with_ends(array, stream_key, least, high):
    place = [jax.random.randint(jax.random.fold_in(stream_key, axis), (), 0, length) for axis, length in enumerate(array.shape)]
    longest = array.shape.index(max(array.shape))
    beside = place[:longest] + [(place[longest] + 1) % array.shape[longest]] + place[longest + 1:]
    return array.at[tuple(place)].set(least).at[tuple(beside)].set(high)


def levels(rng, shape, split, least, top_value):
    factor_of, own = 1.0, jax.random.fold_in(rng, 6)
    for position, shards_of in split:
        heights = jnp.exp(jax.random.uniform(jax.random.fold_in(own, position), (shards_of,), jnp.float32, least / len(split), top_value / len(split)))
        factor_of = factor_of * jnp.repeat(heights, shape[position] // shards_of).reshape([-1 if axis == position else 1 for axis in range(len(shape))])
    return factor_of


def normal_values(own_key, extent, deviation, most, shards=(), kind=jnp.bfloat16):
    array = deviation * jax.random.normal(own_key, extent, jnp.float32)
    if shards:
        array = array * levels(own_key, extent, shards, -0.22, 0.18)
    return jnp.clip(array, -most, most).astype(kind)


def setup_inputs(seed: int = 0) -> dict:
    keys = jax.random.split(jax.random.key(seed), 6)
    return {
        "coef": normal_values(keys[0], (NAO, NOCC), (NAO // 16) ** -0.5, 0.5, ((0, 4), (1, 8))),
        "half_ints": normal_values(keys[1], (NOCC, DOM, NAO), 0.084, 0.5, ((0, 8), (2, 4))),
        "metric_inv": draw_metric_inv(jax.random.fold_in(keys[5], 71), 0),
        "dom_blocks": draw_dom_blocks(jax.random.fold_in(keys[5], 71), 0),
        "dom_len": with_ends(jax.random.randint(keys[4], (NOCC,), DOMB // 4, DOMB + 1), jax.random.fold_in(keys[4], 1), DOMB // 4, DOMB).astype(jnp.int32),
    }


def fit_one(ints_one, blocks_one, length_one, metric_inv):
    metric_rows = metric_inv[blocks_one].astype(jnp.float32)
    raw_ints = ints_one.reshape(DOMB, BLK, NAO).astype(jnp.float32)
    fitted = jnp.einsum('sab,sbm->sam', metric_rows, raw_ints)
    live_slots = jnp.arange(DOMB, dtype=jnp.int32) < length_one
    fitted = jnp.where(live_slots[:, None, None], fitted, 0.0)
    return fitted.reshape(DOM, NAO).astype(jnp.bfloat16)


def reference(coef, half_ints, metric_inv, dom_blocks, dom_len):
    fitted = lax.map(lambda item: fit_one(item[0], item[1], item[2], metric_inv), (half_ints, dom_blocks, dom_len))
    fitted_wide = fitted.astype(jnp.float32)
    pair_sum = jnp.einsum('ipm,mi->ip', fitted_wide, coef.astype(jnp.float32))
    one_hot = (dom_blocks[:, :, None] == jnp.arange(NFITB, dtype=jnp.int32)[None, None, :]).astype(jnp.float32)
    density = jnp.einsum('isf,isr->fr', one_hot, pair_sum.reshape(NOCC, DOMB, BLK)).reshape(NFIT)
    stacked = fitted_wide.reshape(NOCC * DOM, NAO)
    exchange_k = jnp.dot(stacked.T, stacked, preferred_element_type=jnp.float32)
    return exchange_k, density
```

```python
import jax
import jax.numpy as jnp
from jax import lax
from jax.sharding import PartitionSpec as P


def general_plan(coef, half_ints, metric_inv, dom_blocks, dom_len):
    lmo_count, domain, ao_rows = half_ints.shape
    block = metric_inv.shape[1]
    slots = domain // block
    fit_blocks = metric_inv.shape[0]
    metric_rows = metric_inv[dom_blocks]
    raw_ints = half_ints.reshape(lmo_count, slots, block, ao_rows)
    fitted = jnp.einsum(
        "isab,isbm->isam", metric_rows, raw_ints, preferred_element_type=jnp.float32
    )
    live_slots = jnp.arange(slots, dtype=jnp.int32)[None, :] < dom_len[:, None]
    fitted = jnp.where(live_slots[:, :, None, None], fitted, 0.0)
    fitted = fitted.reshape(lmo_count, domain, ao_rows).astype(jnp.bfloat16)
    pair_part = jnp.einsum("ipm,mi->ip", fitted, coef, preferred_element_type=jnp.float32)
    one_hot = (
        dom_blocks[:, :, None] == jnp.arange(fit_blocks, dtype=jnp.int32)[None, None, :]
    ).astype(jnp.float32)
    local_density = jnp.einsum("isf,isr->fr", one_hot, pair_part.reshape(lmo_count, slots, block))
    density = lax.psum(local_density, ("occ", "ao"))
    density = density.reshape(fit_blocks * block)
    partial_value = jnp.einsum(
        "ipm,ipn->mn",
        fitted,
        lax.all_gather(fitted, "ao", axis=2, tiled=True),
        preferred_element_type=jnp.float32,
    )
    exchange_k = lax.psum_scatter(partial_value, "occ", scatter_dimension=1, tiled=True)
    return (exchange_k, density)


def line_plan(n_occ, n_ao):
    last = n_ao - 1
    chips = n_occ // 2

    def device(chip, core, plane):
        return (2 * chip + core) * n_ao + plane

    def pairs(moves):
        return [
            (device(*src[:1], core, src[1]), device(*dst[:1], core, dst[1]))
            for src, dst in moves
            for core in range(2)
        ]

    def far_of(plane):
        return plane ^ 2

    def on_device(coef, half_ints, metric_inv, dom_blocks, dom_len):
        _, domain, ao_rows = half_ints.shape
        fit_blocks, block, _ = metric_inv.shape
        slots = domain // block
        half = ao_rows // 2
        bf16, f32 = jnp.bfloat16, jnp.float32
        plane = lax.axis_index("ao")
        occ = lax.axis_index("occ")
        chip, core = occ // 2, occ % 2
        both = ("occ", "ao")

        raw = half_ints[0]
        left = lax.ppermute(raw, "ao", [(i, i + 1) for i in range(last)])
        right = lax.ppermute(raw, "ao", [(i + 1, i) for i in range(last)])
        from_low = lax.ppermute(left, "ao", [(1, 2), (2, 3)])
        from_high = lax.ppermute(right, "ao", [(1, 0), (2, 1)])

        live = jnp.arange(slots, dtype=jnp.int32) < dom_len[0]
        metric = jnp.where(live[:, None, None], metric_inv[dom_blocks[0]], 0)

        def fit(ints):
            out = jnp.einsum(
                "sab,sbm->sam",
                metric,
                ints.reshape(slots, block, ao_rows),
                preferred_element_type=f32,
            )
            return out.reshape(domain, ao_rows).astype(bf16)

        def product(a, b):
            return jnp.einsum("pm,pn->mn", a, b, preferred_element_type=f32)

        mine = fit(raw)
        pair = jnp.einsum("pm,m->p", mine, coef[:, 0], preferred_element_type=f32)
        one_hot = dom_blocks[0][:, None] == jnp.arange(fit_blocks, dtype=jnp.int32)
        density = jnp.einsum(
            "sf,sr->fr",
            one_hot.astype(f32),
            pair.reshape(slots, block),
            precision=lax.Precision.HIGHEST,
        )
        for axis, n, bit in (("occ", n_occ, 1), ("occ", n_occ, 2), ("occ", n_occ, 4), ("ao", n_ao, 1), ("ao", n_ao, 2)):
            density = density + lax.ppermute(density, axis, [(i, i ^ bit) for i in range(n)])

        def over_cores(blocks):
            keep = lax.dynamic_slice_in_dim(blocks, core * half, half, 2)
            give = lax.dynamic_slice_in_dim(blocks, (1 - core) * half, half, 2)
            got = lax.ppermute(give.astype(bf16), "occ", [(i, i ^ 1) for i in range(n_occ)])
            return keep + got.astype(f32)

        near_left, near_right = fit(left), fit(right)
        near = jnp.stack([product(mine, near_left), product(mine, mine), product(mine, near_right)])
        near = over_cores(near)

        def near_block(target):
            return near[jnp.clip(target - plane + 1, 0, 2)]

        def is_near(p, c):
            return abs(p - c) <= 1

        total = jnp.where(jnp.abs(chip - plane) <= 1, near_block(chip), 0.0)
        for k in range(1, chips):
            moves = [((c, p), (c ^ k, p)) for p in range(n_ao) for c in range(chips) if is_near(p, c ^ k)]
            total = total + lax.ppermute(near_block(chip ^ k).astype(bf16), both, pairs(moves)).astype(f32)

        far_raw = jnp.where(plane >= 2, from_low, from_high)
        far = fit(far_raw)
        beside = jnp.where(plane == 1, near_left, near_right)
        late = over_cores(jnp.stack([product(mine, far), product(beside, far)]))
        target = far_of(plane)
        late_total = jnp.where(chip == target, late[0], late[1])
        for k in range(1, chips):
            moves = [((far_of(p) ^ k, p), (far_of(p), p)) for p in range(n_ao)]
            moves += [((far_of(p) ^ 1 ^ k, p), (far_of(p) ^ 1, p)) for p in (1, 2)]
            give = jnp.where((chip ^ k) == target, late[0], late[1]).astype(bf16)
            late_total = late_total + lax.ppermute(give, both, pairs(moves)).astype(f32)
        ends = [((far_of(p) ^ 1, p), (far_of(p), 0 if p == 1 else last)) for p in (1, 2)]
        end_total = lax.ppermute(late_total.astype(bf16), both, pairs(ends)).astype(f32)
        exchange_k = total + jnp.where(chip == target, late_total, end_total)
        return exchange_k, density.reshape(fit_blocks * block)

    return on_device


def solution(mesh):
    n_occ, n_ao = mesh.shape["occ"], mesh.shape["ao"]
    in_specs = (P("ao", "occ"), P("occ", None, "ao"), P(), P("occ", None), P("occ"))
    out_specs = (P("ao", "occ"), P())

    def whole(*args):
        one_orbital = args[1].shape[0] == n_occ
        fast = n_ao == 4 and n_occ == 2 * n_ao and one_orbital
        body = line_plan(n_occ, n_ao) if fast else general_plan
        return jax.shard_map(
            body, mesh=mesh, in_specs=in_specs, out_specs=out_specs, check_vma=False
        )(*args)

    return whole
```

```python
import jax
import jax.numpy as jnp
from jax import lax
from jax.experimental import pallas as pl
from jax.experimental.pallas import tpu as pltpu
from jax.sharding import PartitionSpec as P


VMEM_LIMIT = 18 * 2**20


def general_plan(coef, half_ints, metric_inv, dom_blocks, dom_len):
    lmo_count, domain, ao_rows = half_ints.shape
    block = metric_inv.shape[1]
    slots = domain // block
    fit_blocks = metric_inv.shape[0]
    metric_rows = metric_inv[dom_blocks]
    raw_ints = half_ints.reshape(lmo_count, slots, block, ao_rows)
    fitted = jnp.einsum(
        "isab,isbm->isam", metric_rows, raw_ints, preferred_element_type=jnp.float32
    )
    live_slots = jnp.arange(slots, dtype=jnp.int32)[None, :] < dom_len[:, None]
    fitted = jnp.where(live_slots[:, :, None, None], fitted, 0.0)
    fitted = fitted.reshape(lmo_count, domain, ao_rows).astype(jnp.bfloat16)
    pair_part = jnp.einsum("ipm,mi->ip", fitted, coef, preferred_element_type=jnp.float32)
    one_hot = (
        dom_blocks[:, :, None] == jnp.arange(fit_blocks, dtype=jnp.int32)[None, None, :]
    ).astype(jnp.float32)
    local_density = jnp.einsum("isf,isr->fr", one_hot, pair_part.reshape(lmo_count, slots, block))
    density = lax.psum(local_density, ("occ", "ao"))
    density = density.reshape(fit_blocks * block)
    partial_value = jnp.einsum(
        "ipm,ipn->mn",
        fitted,
        lax.all_gather(fitted, "ao", axis=2, tiled=True),
        preferred_element_type=jnp.float32,
    )
    exchange_k = lax.psum_scatter(partial_value, "occ", scatter_dimension=1, tiled=True)
    return (exchange_k, density)


def line_plan(n_occ, n_ao):
    chips = n_occ // 2

    def device(chip, core, plane):
        return (2 * chip + core) * n_ao + plane

    def both_cores(moves, swap=0):
        return [
            (device(src[1], core, src[0]), device(dst[1], core ^ swap, dst[0]))
            for src, dst in moves
            for core in range(2)
        ]

    def one_core(moves):
        return [
            (device(chip, core, src), device(chip, core, dst))
            for core, src, dst in moves
            for chip in range(chips)
        ]

    middle = (1, 2)
    spots = [(p, c) for p in range(n_ao) for c in range(chips)]

    def early_owner(p, c):
        return abs(p - c) <= 1 or (p in middle and c == p ^ 2)

    early_turn = [((p, c), (c, p)) for p, c in spots if abs(p - c) == 1] + [((1, 3), (2, 0)), ((2, 0), (3, 1))]
    early_straight = [((1, 3), (0, 2)), ((2, 0), (1, 3))]
    late_turn = [((1, 3), (3, 1)), ((2, 0), (0, 2)), ((1, 2), (3, 0)), ((2, 1), (0, 3))]
    late_straight = [((1, 2), (0, 3)), ((2, 1), (3, 0))]

    def on_device(coef, half_ints, metric_inv, dom_blocks, dom_len):
        _, domain, ao_rows = half_ints.shape
        fit_blocks, block, _ = metric_inv.shape
        slots = domain // block
        half = ao_rows // 2
        bf16, f32 = jnp.bfloat16, jnp.float32
        plane = lax.axis_index("ao")
        occ = lax.axis_index("occ")
        chip, core = occ // 2, occ % 2
        active = (core + plane) % 2 == 1
        place = jnp.stack([plane, chip, core, active.astype(jnp.int32)]).astype(jnp.int32)
        both = ("occ", "ao")
        whole_vmem = pl.BlockSpec(memory_space=pltpu.VMEM)
        whole_smem = pl.BlockSpec(memory_space=pltpu.SMEM)

        def send(x, pairs):
            return lax.ppermute(x, both, pairs)

        def call(body, inputs, outputs, scratch=(), flops=0, moved=0, far_inputs=0, out_space=None):
            near_inputs = len(inputs) - far_inputs
            return pl.pallas_call(
                body,
                out_shape=[jax.ShapeDtypeStruct(s, d) for s, d in outputs],
                in_specs=[whole_smem] + [whole_vmem] * near_inputs + [hbm] * far_inputs,
                out_specs=[out_space or whole_vmem] * len(outputs),
                scratch_shapes=list(scratch),
                cost_estimate=pl.CostEstimate(flops=flops, bytes_accessed=moved, transcendentals=0),
                compiler_params=pltpu.CompilerParams(vmem_limit_bytes=VMEM_LIMIT),
            )(place, *inputs)

        hbm = pl.BlockSpec(memory_space=pl.ANY)
        in_hbm = pl.BlockSpec(memory_space=pltpu.HBM)

        def group_copies(source, to, sems):
            rows = [pl.ds(g * group, group) for g in range(groups)]
            return [pltpu.make_async_copy(source.at[r, :], to.at[r, :], sems.at[g]) for g, r in enumerate(rows)]

        def fit_in_place(metric_ref, ints_ref, copies, turned_ref=None):
            for g, copy in enumerate(copies):
                copy.wait()
                rows = slice(g * group, (g + 1) * group)
                value = jnp.dot(metric_ref[g], ints_ref[rows, :], preferred_element_type=f32).astype(bf16)
                ints_ref[rows, :] = value
                if turned_ref is not None:
                    turned_ref[:, rows] = value.T

        def put_halves(at, stage_ref, own_hbm, give_hbm, j, sems, act):
            for h in range(2):
                part = stage_ref.at[j, :, pl.ds(h * half, half)]

                @pl.when(at[2] == h)
                def _():
                    act(pltpu.make_async_copy(part, own_hbm.at[j], sems.at[j, h]))

                @pl.when(at[2] != h)
                def _():
                    act(pltpu.make_async_copy(part, give_hbm.at[j], sems.at[j, h]))

        def start(copy):
            copy.start()

        def wait(copy):
            copy.wait()

        def product(turned_ref, right_ref):
            return jnp.dot(turned_ref[...], right_ref[...], preferred_element_type=f32).astype(bf16)

        raw = half_ints[0]
        low = send(raw, one_core([(0, 0, 1), (0, 2, 3), (1, 1, 2)]))
        high = send(raw, one_core([(0, 2, 1), (1, 1, 0), (1, 3, 2)]))
        far = send(raw, one_core([(0, 3, 1), (1, 0, 2)]))

        live = jnp.arange(slots, dtype=jnp.int32) < dom_len[0]
        metric = jnp.where(live[:, None, None], metric_inv[dom_blocks[0]], 0)
        wide = 2 if slots % 2 == 0 else 1
        groups, group = slots // wide, wide * block
        on_diagonal = jnp.eye(wide, dtype=bool)[None, :, None, :, None]
        metric_wide = jnp.where(
            on_diagonal, metric.reshape(groups, wide, block, 1, block), jnp.zeros((), bf16)
        ).reshape(groups, group, group)
        mine = (
            jnp.einsum("sab,sbm->sam", metric, raw.reshape(slots, block, ao_rows), preferred_element_type=f32)
            .reshape(domain, ao_rows)
            .astype(bf16)
        )
        mine_turned = mine.T
        pair = jnp.einsum("pm,m->p", mine, coef[:, 0], preferred_element_type=f32)
        one_hot = dom_blocks[0][:, None] == jnp.arange(fit_blocks, dtype=jnp.int32)
        density = jnp.einsum(
            "sf,sr->fr",
            one_hot.astype(f32),
            pair.reshape(slots, block),
            precision=lax.Precision.HIGHEST,
        )
        for axis, n, bit in (("occ", n_occ, 1), ("occ", n_occ, 2), ("occ", n_occ, 4), ("ao", n_ao, 1), ("ao", n_ao, 2)):
            density = density + lax.ppermute(density, axis, [(i, i ^ bit) for i in range(n)])

        square = jnp.einsum("pm,pn->mn", mine, mine, preferred_element_type=f32)
        keep = lax.dynamic_slice_in_dim(square, core * half, half, 1)
        give = lax.dynamic_slice_in_dim(square, (1 - core) * half, half, 1).astype(bf16)
        swap = [(i, i ^ 1) for i in range(n_occ)]
        got = lax.ppermute(give, "occ", swap)
        square = (keep + got.astype(f32)).astype(bf16)
        to_sibling = [(device(c, (p + 1) % 2, p), device(c, p % 2, p)) for p in range(n_ao) for c in range(chips)]

        def near_body(
            at, metric_ref, turned_ref, low_hbm, high_hbm,
            own_hbm, give_hbm, outer_hbm,
            low_ref, high_ref, low_turned, high_turned, stage, in_sems, out_sems, outer_sem,
        ):
            plane_now, busy = at[0], at[3] == 1
            has_low, has_high = busy & (plane_now >= 1), busy & (plane_now <= n_ao - 2)
            low_copies = group_copies(low_hbm, low_ref, in_sems.at[0])
            high_copies = group_copies(high_hbm, high_ref, in_sems.at[1])

            @pl.when(has_low)
            def _():
                for copy in low_copies:
                    copy.start()

            @pl.when(has_high)
            def _():
                for copy in high_copies:
                    copy.start()

            @pl.when(has_low)
            def _():
                fit_in_place(metric_ref, low_ref, low_copies, low_turned)
                stage[0] = product(turned_ref, low_ref)
                put_halves(at, stage, own_hbm, give_hbm, 0, out_sems, start)

            @pl.when(has_high)
            def _():
                fit_in_place(metric_ref, high_ref, high_copies, high_turned)
                stage[1] = product(turned_ref, high_ref)
                put_halves(at, stage, own_hbm, give_hbm, 1, out_sems, start)

            low_outer = pltpu.make_async_copy(low_turned, outer_hbm, outer_sem)
            high_outer = pltpu.make_async_copy(high_turned, outer_hbm, outer_sem)

            @pl.when(has_low & has_high)
            def _():
                @pl.when(plane_now == 1)
                def _():
                    low_outer.start()

                @pl.when(plane_now != 1)
                def _():
                    high_outer.start()

                stage[2] = product(low_turned, high_ref)
                put_halves(at, stage, own_hbm, give_hbm, 2, out_sems, start)

            @pl.when(has_low)
            def _():
                put_halves(at, stage, own_hbm, give_hbm, 0, out_sems, wait)

            @pl.when(has_high)
            def _():
                put_halves(at, stage, own_hbm, give_hbm, 1, out_sems, wait)

            @pl.when(has_low & has_high)
            def _():
                low_outer.wait()
                put_halves(at, stage, own_hbm, give_hbm, 2, out_sems, wait)

        piece = (ao_rows, half)
        fitted = (domain, ao_rows)
        product_flops = 2 * domain * ao_rows * ao_rows
        square_tile = (ao_rows, ao_rows)
        own, give, outer = call(
            near_body,
            [metric_wide, mine_turned, low, high],
            [((3, *piece), bf16), ((3, *piece), bf16), (fitted[::-1], bf16)],
            [
                pltpu.VMEM(fitted, bf16),
                pltpu.VMEM(fitted, bf16),
                pltpu.VMEM(fitted[::-1], bf16),
                pltpu.VMEM(fitted[::-1], bf16),
                pltpu.VMEM((3, *square_tile), bf16),
                pltpu.SemaphoreType.DMA((2, groups)),
                pltpu.SemaphoreType.DMA((3, 2)),
                pltpu.SemaphoreType.DMA,
            ],
            3 * product_flops,
            6 * 2**20,
            far_inputs=2,
            out_space=in_hbm,
        )
        got = send(give, to_sibling)

        def pick(own_all, got_all, alone, index_of):
            count = own_all.shape[0]

            def body(at, own_hbm, got_hbm, alone_hbm, *rest):
                outs, sems = rest[:chips], rest[chips]
                busy = at[3] == 1
                for k in range(chips):
                    j = index_of(at[0], at[1] ^ k)
                    safe = jnp.clip(j, 0, count - 1)
                    mine_copy = pltpu.make_async_copy(own_hbm.at[safe], outs[k], sems.at[k])
                    got_copy = pltpu.make_async_copy(got_hbm.at[safe], outs[k], sems.at[k])
                    alone_copy = pltpu.make_async_copy(alone_hbm, outs[k], sems.at[k])

                    @pl.when((j >= 0) & busy)
                    def _():
                        mine_copy.start()

                    @pl.when((j >= 0) & jnp.logical_not(busy))
                    def _():
                        got_copy.start()

                    @pl.when(j < 0)
                    def _():
                        alone_copy.start()

                for k in range(chips):
                    pltpu.make_async_copy(alone_hbm, outs[k], sems.at[k]).wait()

            return call(
                body,
                [own_all, got_all, alone],
                [(piece, bf16)] * chips,
                [pltpu.SemaphoreType.DMA((chips,))],
                0,
                2 * 2**20,
                far_inputs=3,
            )

        def early_index(plane_now, goal):
            away = goal - plane_now
            one = jnp.where(away == -1, 0, jnp.where(away == 1, 1, 2))
            return jnp.where(away == 0, -1, one)

        picked = pick(own, got, square, early_index)
        early_in = [picked[0]]
        for k in range(1, chips):
            moves = [((p, c ^ k), (p, c)) for p, c in spots if early_owner(p, c)]
            early_in.append(send(picked[k], both_cores(moves)))

        def sum_body(at, a_ref, b_ref, c_ref, d_ref, total_ref, same_ref, other_ref, full):
            core_now = at[2]
            full[...] = (
                a_ref[...].astype(f32) + b_ref[...].astype(f32) + c_ref[...].astype(f32) + d_ref[...].astype(f32)
            )
            total_ref[...] = full[...].astype(bf16)
            for h in range(2):
                turned = full[h * half : (h + 1) * half, :].T.astype(bf16)

                @pl.when(core_now == h)
                def _():
                    same_ref[...] = turned

                @pl.when(core_now != h)
                def _():
                    other_ref[...] = turned

        corner = (half, half)

        def sum_up(parts):
            return call(
                sum_body, parts, [(piece, bf16), (corner, bf16), (corner, bf16)], [pltpu.VMEM(piece, f32)], 0, 2 * 2**20
            )

        early, early_same, early_other = sum_up(early_in)

        def far_body(
            at, metric_ref, turned_ref, outer_hbm, far_hbm,
            own_hbm, give_hbm,
            far_ref, outer_ref, stage, in_sems, out_sems, outer_sem,
        ):
            copies = group_copies(far_hbm, far_ref, in_sems)
            outer_copy = pltpu.make_async_copy(outer_hbm, outer_ref, outer_sem)

            @pl.when((at[3] == 1) & (at[0] >= 1) & (at[0] <= n_ao - 2))
            def _():
                for copy in copies:
                    copy.start()
                outer_copy.start()
                fit_in_place(metric_ref, far_ref, copies)
                stage[0] = product(turned_ref, far_ref)
                put_halves(at, stage, own_hbm, give_hbm, 0, out_sems, start)
                outer_copy.wait()
                stage[1] = product(outer_ref, far_ref)
                put_halves(at, stage, own_hbm, give_hbm, 1, out_sems, start)
                put_halves(at, stage, own_hbm, give_hbm, 0, out_sems, wait)
                put_halves(at, stage, own_hbm, give_hbm, 1, out_sems, wait)

        late_own, late_give = call(
            far_body,
            [metric_wide, mine_turned, outer, far],
            [((2, *piece), bf16), ((2, *piece), bf16)],
            [
                pltpu.VMEM(fitted, bf16),
                pltpu.VMEM(fitted[::-1], bf16),
                pltpu.VMEM((2, *square_tile), bf16),
                pltpu.SemaphoreType.DMA((groups,)),
                pltpu.SemaphoreType.DMA((2, 2)),
                pltpu.SemaphoreType.DMA,
            ],
            2 * product_flops,
            4 * 2**20,
            far_inputs=2,
            out_space=in_hbm,
        )
        late_pairs = [(device(c, (p + 1) % 2, p), device(c, p % 2, p)) for p in middle for c in range(chips)]
        late_got = send(late_give, late_pairs)

        def late_index(plane_now, goal):
            return jnp.where(goal == plane_now ^ 2, 0, 1)

        picked = pick(late_own, late_got, square, late_index)
        late_in = [picked[0]]
        for k in range(1, chips):
            moves = [((p, p ^ 2 ^ k), (p, p ^ 2)) for p in middle]
            moves += [((p, p ^ 3 ^ k), (p, p ^ 3)) for p in middle]
            late_in.append(send(picked[k], both_cores(moves)))
        late, late_same, late_other = sum_up(late_in)

        arrived = [
            send(early_same, both_cores(early_turn)),
            send(early_other, both_cores(early_turn, 1)),
            send(early, both_cores(early_straight)),
            send(late_same, both_cores(late_turn)),
            send(late_other, both_cores(late_turn, 1)),
            send(late, both_cores(late_straight)),
        ]

        def last_body(at, early_ref, late_ref, es, eo, ed, ls, lo, ld, out_ref):
            plane_now, chip_now, core_now = at[0], at[1], at[2]
            gap = jnp.abs(plane_now - chip_now)
            in_middle = (plane_now >= 1) & (plane_now <= n_ao - 2)
            out_ref[...] = ed[...].astype(f32) + ld[...].astype(f32)

            @pl.when(gap <= 1)
            def _():
                out_ref[...] += early_ref[...].astype(f32)

            @pl.when((gap == 2) & in_middle)
            def _():
                out_ref[...] += late_ref[...].astype(f32)

            same_rows = pl.ds(pl.multiple_of(core_now * half, half), half)
            other_rows = pl.ds(pl.multiple_of((1 - core_now) * half, half), half)
            out_ref[same_rows, :] += es[...].astype(f32) + ls[...].astype(f32)
            out_ref[other_rows, :] += eo[...].astype(f32) + lo[...].astype(f32)

        (exchange_k,) = call(last_body, [early, late, *arrived], [(piece, f32)], [], 0, 3 * 2**20)
        return exchange_k, density.reshape(fit_blocks * block)

    return on_device


def solution(mesh):
    n_occ, n_ao = mesh.shape["occ"], mesh.shape["ao"]
    in_specs = (P("ao", "occ"), P("occ", None, "ao"), P(), P("occ", None), P("occ"))
    out_specs = (P("ao", "occ"), P())

    def sharded(body):
        return jax.shard_map(body, mesh=mesh, in_specs=in_specs, out_specs=out_specs, check_vma=False)

    if not (n_ao == 4 and n_occ == 2 * n_ao):
        return sharded(general_plan)

    def whole(*args):
        if args[1].shape[0] != n_occ:
            return sharded(general_plan)(*args)
        return sharded(line_plan(n_occ, n_ao))(*args)

    return whole
```

```python
import jax
import jax.numpy as jnp
from jax import lax
from jax.experimental import pallas as pl
from jax.experimental.pallas import tpu as pltpu
from jax.sharding import PartitionSpec as P


VMEM_LIMIT = 18 * 2**20


def general_plan(coef, half_ints, metric_inv, dom_blocks, dom_len):
    lmo_count, domain, ao_rows = half_ints.shape
    block = metric_inv.shape[1]
    slots = domain // block
    fit_blocks = metric_inv.shape[0]
    metric_rows = metric_inv[dom_blocks]
    raw_ints = half_ints.reshape(lmo_count, slots, block, ao_rows)
    fitted = jnp.einsum(
        "isab,isbm->isam", metric_rows, raw_ints, preferred_element_type=jnp.float32
    )
    live_slots = jnp.arange(slots, dtype=jnp.int32)[None, :] < dom_len[:, None]
    fitted = jnp.where(live_slots[:, :, None, None], fitted, 0.0)
    fitted = fitted.reshape(lmo_count, domain, ao_rows).astype(jnp.bfloat16)
    pair_part = jnp.einsum("ipm,mi->ip", fitted, coef, preferred_element_type=jnp.float32)
    one_hot = (
        dom_blocks[:, :, None] == jnp.arange(fit_blocks, dtype=jnp.int32)[None, None, :]
    ).astype(jnp.float32)
    local_density = jnp.einsum("isf,isr->fr", one_hot, pair_part.reshape(lmo_count, slots, block))
    density = lax.psum(local_density, ("occ", "ao"))
    density = density.reshape(fit_blocks * block)
    partial_value = jnp.einsum(
        "ipm,ipn->mn",
        fitted,
        lax.all_gather(fitted, "ao", axis=2, tiled=True),
        preferred_element_type=jnp.float32,
    )
    exchange_k = lax.psum_scatter(partial_value, "occ", scatter_dimension=1, tiled=True)
    return (exchange_k, density)


def line_plan(n_occ, n_ao):
    chips = n_occ // 2

    def device(chip, core, plane):
        return (2 * chip + core) * n_ao + plane

    def both_cores(moves, swap=0):
        return [
            (device(src[1], core, src[0]), device(dst[1], core ^ swap, dst[0]))
            for src, dst in moves
            for core in range(2)
        ]

    def one_core(moves):
        return [
            (device(chip, core, src), device(chip, core, dst))
            for core, src, dst in moves
            for chip in range(chips)
        ]

    spots = [(p, c) for p in range(n_ao) for c in range(chips)]

    far_turn = [((1, 3), (3, 1)), ((2, 0), (0, 2))]
    near_turn = [((p, c), (c, p)) for p, c in spots if abs(p - c) == 1]
    near_turn += [((1, 3), (2, 0)), ((2, 0), (3, 1)), ((1, 1), (3, 0)), ((2, 2), (0, 3))]
    near_straight = [((1, 3), (0, 2)), ((2, 0), (1, 3)), ((1, 1), (0, 3)), ((2, 2), (3, 0))]

    def on_device(coef, half_ints, metric_inv, dom_blocks, dom_len):
        _, domain, ao_rows = half_ints.shape
        fit_blocks, block, _ = metric_inv.shape
        slots = domain // block
        half = ao_rows // 2
        bf16, f32 = jnp.bfloat16, jnp.float32
        plane = lax.axis_index("ao")
        occ = lax.axis_index("occ")
        chip, core = occ // 2, occ % 2
        active = (core + plane) % 2 == 1
        place = jnp.stack([plane, chip, core, active.astype(jnp.int32)]).astype(jnp.int32)
        both = ("occ", "ao")
        whole_vmem = pl.BlockSpec(memory_space=pltpu.VMEM)
        whole_smem = pl.BlockSpec(memory_space=pltpu.SMEM)

        def send(x, pairs):
            return lax.ppermute(x, both, pairs)

        def call(body, inputs, outputs, scratch=(), flops=0, moved=0, far_inputs=0, out_space=None):
            near_inputs = len(inputs) - far_inputs
            return pl.pallas_call(
                body,
                out_shape=[jax.ShapeDtypeStruct(s, d) for s, d in outputs],
                in_specs=[whole_smem] + [whole_vmem] * near_inputs + [hbm] * far_inputs,
                out_specs=[out_space or whole_vmem] * len(outputs),
                scratch_shapes=list(scratch),
                cost_estimate=pl.CostEstimate(flops=flops, bytes_accessed=moved, transcendentals=0),
                compiler_params=pltpu.CompilerParams(vmem_limit_bytes=VMEM_LIMIT),
            )(place, *inputs)

        hbm = pl.BlockSpec(memory_space=pl.ANY)
        in_hbm = pl.BlockSpec(memory_space=pltpu.HBM)

        def group_copies(source, to, sems):
            rows = [pl.ds(g * group, group) for g in range(groups)]
            return [pltpu.make_async_copy(source.at[r, :], to.at[r, :], sems.at[g]) for g, r in enumerate(rows)]

        def fit_in_place(metric_ref, ints_ref, copies, turned_ref=None):
            for g, copy in enumerate(copies):
                copy.wait()
                rows = slice(g * group, (g + 1) * group)
                value = jnp.dot(metric_ref[g], ints_ref[rows, :], preferred_element_type=f32).astype(bf16)
                ints_ref[rows, :] = value
                if turned_ref is not None:
                    turned_ref[:, rows] = value.T

        def put_halves(at, stage_ref, own_hbm, give_hbm, j, sems, act):
            for h in range(2):
                part = stage_ref.at[j, :, pl.ds(h * half, half)]

                @pl.when(at[2] == h)
                def _():
                    act(pltpu.make_async_copy(part, own_hbm.at[j], sems.at[j, h]))

                @pl.when(at[2] != h)
                def _():
                    act(pltpu.make_async_copy(part, give_hbm.at[j], sems.at[j, h]))

        def start(copy):
            copy.start()

        def wait(copy):
            copy.wait()

        def product(turned_ref, right_ref):
            return jnp.dot(turned_ref[...], right_ref[...], preferred_element_type=f32).astype(bf16)

        raw = half_ints[0]
        low = send(raw, one_core([(0, 0, 1), (0, 2, 3), (1, 1, 2)]))
        high = send(raw, one_core([(0, 2, 1), (1, 1, 0), (1, 3, 2)]))
        far = send(raw, one_core([(0, 3, 1), (1, 0, 2)]))

        live = jnp.arange(slots, dtype=jnp.int32) < dom_len[0]
        metric = jnp.where(live[:, None, None], metric_inv[dom_blocks[0]], 0)
        wide = 2 if slots % 2 == 0 else 1
        groups, group = slots // wide, wide * block
        on_diagonal = jnp.eye(wide, dtype=bool)[None, :, None, :, None]
        metric_wide = jnp.where(
            on_diagonal, metric.reshape(groups, wide, block, 1, block), jnp.zeros((), bf16)
        ).reshape(groups, group, group)
        piece = (ao_rows, half)
        fitted = (domain, ao_rows)
        product_flops = 2 * domain * ao_rows * ao_rows

        def own_body(at, metric_ref, coef_ref, raw_hbm, turned_ref, keep_ref, give_ref, pair_ref, mine_ref, sems):
            copies = group_copies(raw_hbm, mine_ref, sems)
            for copy in copies:
                copy.start()
            fit_in_place(metric_ref, mine_ref, copies, turned_ref)
            value = jnp.dot(turned_ref[...], mine_ref[...], preferred_element_type=f32)
            for h in range(2):
                part = value[:, h * half : (h + 1) * half]

                @pl.when(at[2] == h)
                def _():
                    keep_ref[...] = part

                @pl.when(at[2] != h)
                def _():
                    give_ref[...] = part.astype(bf16)

            pair_ref[...] = jnp.dot(coef_ref[...], turned_ref[...], preferred_element_type=f32)

        lines = 16
        mine_turned, square_keep, square_give, pair = call(
            own_body,
            [metric_wide, jnp.broadcast_to(coef.T, (lines, ao_rows)), raw],
            [(fitted[::-1], bf16), (piece, f32), (piece, bf16), ((lines, domain), f32)],
            [pltpu.VMEM(fitted, bf16), pltpu.SemaphoreType.DMA((groups,))],
            product_flops,
            4 * 2**20,
            far_inputs=1,
        )
        swap = [(i, i ^ 1) for i in range(n_occ)]
        square_got = lax.ppermute(square_give, "occ", swap)
        one_hot = dom_blocks[0][:, None] == jnp.arange(fit_blocks, dtype=jnp.int32)
        density = jnp.einsum(
            "sf,sr->fr",
            one_hot.astype(f32),
            pair[0].reshape(slots, block),
            precision=lax.Precision.HIGHEST,
        )
        for axis, n, bit in (("occ", n_occ, 1), ("occ", n_occ, 2), ("occ", n_occ, 4), ("ao", n_ao, 1), ("ao", n_ao, 2)):
            density = density + lax.ppermute(density, axis, [(i, i ^ bit) for i in range(n)])

        square_tile = (ao_rows, ao_rows)

        def far_body(
            at, metric_ref, turned_ref, far_hbm,
            own_hbm, give_hbm, fit_hbm,
            far_ref, stage, in_sems, out_sems, fit_sem,
        ):
            copies = group_copies(far_hbm, far_ref, in_sems)

            @pl.when((at[3] == 1) & (at[0] >= 1) & (at[0] <= n_ao - 2))
            def _():
                for copy in copies:
                    copy.start()
                fit_in_place(metric_ref, far_ref, copies)
                fit_out = pltpu.make_async_copy(far_ref, fit_hbm, fit_sem)
                fit_out.start()
                stage[0] = product(turned_ref, far_ref)
                put_halves(at, stage, own_hbm, give_hbm, 0, out_sems, start)
                fit_out.wait()
                put_halves(at, stage, own_hbm, give_hbm, 0, out_sems, wait)

        far_own, far_give, far_fit = call(
            far_body,
            [metric_wide, mine_turned, far],
            [((1, *piece), bf16), ((1, *piece), bf16), (fitted, bf16)],
            [
                pltpu.VMEM(fitted, bf16),
                pltpu.VMEM((1, *square_tile), bf16),
                pltpu.SemaphoreType.DMA((groups,)),
                pltpu.SemaphoreType.DMA((1, 2)),
                pltpu.SemaphoreType.DMA,
            ],
            product_flops,
            4 * 2**20,
            far_inputs=1,
            out_space=in_hbm,
        )
        far_got = lax.ppermute(far_give, "occ", swap)

        def exchange(pieces):
            parts = [pieces[0]]
            for k in range(1, chips):
                parts.append(lax.ppermute(pieces[k], "occ", [(i, i ^ (2 * k)) for i in range(n_occ)]))
            return parts

        def pick(own_all, got_all, index_of, square_parts=()):
            count = own_all.shape[0]

            def body(at, *refs):
                parts, (own_hbm, got_hbm), rest = refs[: len(square_parts)], refs[len(square_parts) :][:2], refs[len(square_parts) + 2 :]
                outs, sems = rest[:chips], rest[chips]
                busy = at[3] == 1
                steps = []
                for k in range(chips):
                    j = index_of(at[0], at[1] ^ k)
                    safe = jnp.clip(j, 0, count - 1)
                    from_own = pltpu.make_async_copy(own_hbm.at[safe], outs[k], sems.at[k])
                    from_got = pltpu.make_async_copy(got_hbm.at[safe], outs[k], sems.at[k])
                    steps.append((j, from_own, from_got))

                    @pl.when((j >= 0) & busy)
                    def _():
                        from_own.start()

                    @pl.when((j >= 0) & jnp.logical_not(busy))
                    def _():
                        from_got.start()

                for k, (j, from_own, _) in enumerate(steps):
                    if parts:

                        @pl.when(j < 0)
                        def _():
                            outs[k][...] = (parts[0][...] + parts[1][...].astype(f32)).astype(bf16)

                    @pl.when(j >= 0)
                    def _():
                        from_own.wait()

            return call(
                body,
                [*square_parts, own_all, got_all],
                [(piece, bf16)] * chips,
                [pltpu.SemaphoreType.DMA((chips,))],
                0,
                2 * 2**20,
                far_inputs=2,
            )

        def far_index(plane_now, goal):
            return jnp.where(goal == plane_now, -1, 0)

        picked = pick(far_own, far_got, far_index, (square_keep, square_got))
        far_parts = exchange(picked)

        def sum_body(at, a_ref, b_ref, c_ref, d_ref, total_ref, same_ref, other_ref, full):
            core_now = at[2]
            full[...] = (
                a_ref[...].astype(f32) + b_ref[...].astype(f32) + c_ref[...].astype(f32) + d_ref[...].astype(f32)
            )
            total_ref[...] = full[...].astype(bf16)
            for h in range(2):
                turned = full[h * half : (h + 1) * half, :].T.astype(bf16)

                @pl.when(core_now == h)
                def _():
                    same_ref[...] = turned

                @pl.when(core_now != h)
                def _():
                    other_ref[...] = turned

        corner = (half, half)

        def sum_up(parts):
            return call(
                sum_body, parts, [(piece, bf16), (corner, bf16), (corner, bf16)], [pltpu.VMEM(piece, f32)], 0, 2 * 2**20
            )

        far_total, far_same, far_other = sum_up(far_parts)

        def near_body(
            at, metric_ref, turned_hbm, low_hbm, high_hbm, fit_hbm,
            own_hbm, give_hbm,
            low_ref, high_ref, far_ref, low_turned, high_turned, turned_ref, stage, in_sems, out_sems, more_sems,
        ):
            plane_now, busy = at[0], at[3] == 1
            has_low, has_high = busy & (plane_now >= 1), busy & (plane_now <= n_ao - 2)
            inner = has_low & has_high
            low_copies = group_copies(low_hbm, low_ref, in_sems.at[0])
            high_copies = group_copies(high_hbm, high_ref, in_sems.at[1])
            turned_copy = pltpu.make_async_copy(turned_hbm, turned_ref, more_sems.at[0])
            far_copy = pltpu.make_async_copy(fit_hbm, far_ref, more_sems.at[1])

            @pl.when(has_low)
            def _():
                for copy in low_copies:
                    copy.start()

            @pl.when(busy)
            def _():
                turned_copy.start()

            @pl.when(has_high)
            def _():
                for copy in high_copies:
                    copy.start()

            @pl.when(inner)
            def _():
                far_copy.start()

            @pl.when(has_low)
            def _():
                fit_in_place(metric_ref, low_ref, low_copies, low_turned)

            @pl.when(busy)
            def _():
                turned_copy.wait()

            @pl.when(has_low)
            def _():
                stage[0] = product(turned_ref, low_ref)
                put_halves(at, stage, own_hbm, give_hbm, 0, out_sems, start)

            @pl.when(has_high)
            def _():
                fit_in_place(metric_ref, high_ref, high_copies, high_turned)
                stage[1] = product(turned_ref, high_ref)
                put_halves(at, stage, own_hbm, give_hbm, 1, out_sems, start)

            @pl.when(inner)
            def _():
                stage[2] = product(low_turned, high_ref)
                put_halves(at, stage, own_hbm, give_hbm, 2, out_sems, start)
                far_copy.wait()

                @pl.when(plane_now == 1)
                def _():
                    stage[3] = product(low_turned, far_ref)

                @pl.when(plane_now != 1)
                def _():
                    stage[3] = product(high_turned, far_ref)

                put_halves(at, stage, own_hbm, give_hbm, 3, out_sems, start)

            @pl.when(has_low)
            def _():
                put_halves(at, stage, own_hbm, give_hbm, 0, out_sems, wait)

            @pl.when(has_high)
            def _():
                put_halves(at, stage, own_hbm, give_hbm, 1, out_sems, wait)

            @pl.when(inner)
            def _():
                put_halves(at, stage, own_hbm, give_hbm, 2, out_sems, wait)
                put_halves(at, stage, own_hbm, give_hbm, 3, out_sems, wait)

        near_own, near_give = call(
            near_body,
            [metric_wide, mine_turned, low, high, far_fit],
            [((4, *piece), bf16), ((4, *piece), bf16)],
            [
                pltpu.VMEM(fitted, bf16),
                pltpu.VMEM(fitted, bf16),
                pltpu.VMEM(fitted, bf16),
                pltpu.VMEM(fitted[::-1], bf16),
                pltpu.VMEM(fitted[::-1], bf16),
                pltpu.VMEM(fitted[::-1], bf16),
                pltpu.VMEM((4, *square_tile), bf16),
                pltpu.SemaphoreType.DMA((2, groups)),
                pltpu.SemaphoreType.DMA((4, 2)),
                pltpu.SemaphoreType.DMA((2,)),
            ],
            4 * product_flops,
            8 * 2**20,
            far_inputs=4,
            out_space=in_hbm,
        )
        near_got = lax.ppermute(near_give, "occ", swap)

        def near_index(plane_now, goal):
            away = goal - plane_now
            beside = jnp.where(away == -1, 0, 1)
            return jnp.where(jnp.abs(away) == 1, beside, jnp.where(away == 0, 3, 2))

        picked = pick(near_own, near_got, near_index)
        near_total, near_same, near_other = sum_up(exchange(picked))

        arrived = [
            send(near_same, both_cores(near_turn)),
            send(near_other, both_cores(near_turn, 1)),
            send(near_total, both_cores(near_straight)),
            send(far_same, both_cores(far_turn)),
            send(far_other, both_cores(far_turn, 1)),
        ]

        def last_body(at, near_ref, far_ref, ns, no, nd, fs, fo, out_ref):
            plane_now, chip_now, core_now = at[0], at[1], at[2]
            gap = jnp.abs(plane_now - chip_now)
            in_middle = (plane_now >= 1) & (plane_now <= n_ao - 2)
            out_ref[...] = nd[...].astype(f32)

            @pl.when(gap == 1)
            def _():
                out_ref[...] += near_ref[...].astype(f32)

            @pl.when((gap == 0) | ((gap == 2) & in_middle))
            def _():
                out_ref[...] += far_ref[...].astype(f32)

            same_rows = pl.ds(pl.multiple_of(core_now * half, half), half)
            other_rows = pl.ds(pl.multiple_of((1 - core_now) * half, half), half)
            out_ref[same_rows, :] += ns[...].astype(f32) + fs[...].astype(f32)
            out_ref[other_rows, :] += no[...].astype(f32) + fo[...].astype(f32)

        (exchange_k,) = call(last_body, [near_total, far_total, *arrived], [(piece, f32)], [], 0, 3 * 2**20)
        return exchange_k, density.reshape(fit_blocks * block)

    return on_device


def solution(mesh):
    n_occ, n_ao = mesh.shape["occ"], mesh.shape["ao"]
    in_specs = (P("ao", "occ"), P("occ", None, "ao"), P(), P("occ", None), P("occ"))
    out_specs = (P("ao", "occ"), P())

    def sharded(body):
        return jax.shard_map(body, mesh=mesh, in_specs=in_specs, out_specs=out_specs, check_vma=False)

    if not (n_ao == 4 and n_occ == 2 * n_ao):
        return sharded(general_plan)

    def whole(*args):
        if args[1].shape[0] != n_occ:
            return sharded(general_plan)(*args)
        return sharded(line_plan(n_occ, n_ao))(*args)

    return whole
```

```python
import jax
import jax.numpy as jnp
from jax import lax
from jax.experimental import pallas as pl
from jax.experimental.pallas import tpu as pltpu
from jax.sharding import PartitionSpec as P


VMEM_LIMIT = 18 * 2**20


def general_plan(coef, half_ints, metric_inv, dom_blocks, dom_len):
    lmo_count, domain, ao_rows = half_ints.shape
    block = metric_inv.shape[1]
    slots = domain // block
    fit_blocks = metric_inv.shape[0]
    metric_rows = metric_inv[dom_blocks]
    raw_ints = half_ints.reshape(lmo_count, slots, block, ao_rows)
    fitted = jnp.einsum(
        "isab,isbm->isam", metric_rows, raw_ints, preferred_element_type=jnp.float32
    )
    live_slots = jnp.arange(slots, dtype=jnp.int32)[None, :] < dom_len[:, None]
    fitted = jnp.where(live_slots[:, :, None, None], fitted, 0.0)
    fitted = fitted.reshape(lmo_count, domain, ao_rows).astype(jnp.bfloat16)
    pair_part = jnp.einsum("ipm,mi->ip", fitted, coef, preferred_element_type=jnp.float32)
    one_hot = (
        dom_blocks[:, :, None] == jnp.arange(fit_blocks, dtype=jnp.int32)[None, None, :]
    ).astype(jnp.float32)
    local_density = jnp.einsum("isf,isr->fr", one_hot, pair_part.reshape(lmo_count, slots, block))
    density = lax.psum(local_density, ("occ", "ao"))
    density = density.reshape(fit_blocks * block)
    partial_value = jnp.einsum(
        "ipm,ipn->mn",
        fitted,
        lax.all_gather(fitted, "ao", axis=2, tiled=True),
        preferred_element_type=jnp.float32,
    )
    exchange_k = lax.psum_scatter(partial_value, "occ", scatter_dimension=1, tiled=True)
    return (exchange_k, density)


def line_plan(n_occ, n_ao):
    chips = n_occ // 2

    def device(chip, core, plane):
        return (2 * chip + core) * n_ao + plane

    def both_cores(moves):
        return [
            (device(src[1], core, src[0]), device(dst[1], core, dst[0]))
            for src, dst in moves
            for core in range(2)
        ]

    def one_core(moves):
        return [
            (device(chip, core, src), device(chip, core, dst))
            for core, src, dst in moves
            for chip in range(chips)
        ]

    spots = [(p, c) for p in range(n_ao) for c in range(chips)]

    far_turn = [((1, 3), (3, 1)), ((2, 0), (0, 2))]
    copies = {(0, 1): (0, 2), (3, 2): (3, 1)}
    near_turn = [(copies.get((p, c), (p, c)), (c, p)) for p, c in spots if abs(p - c) == 1]
    near_turn += [((1, 3), (2, 0)), ((2, 0), (3, 1)), ((1, 1), (3, 0)), ((2, 2), (0, 3))]
    near_straight = [((1, 3), (0, 2)), ((2, 0), (1, 3)), ((1, 1), (0, 3)), ((2, 2), (3, 0))]

    def on_device(coef, half_ints, metric_inv, dom_blocks, dom_len):
        _, domain, ao_rows = half_ints.shape
        fit_blocks, block, _ = metric_inv.shape
        slots = domain // block
        half = ao_rows // 2
        bf16, f32 = jnp.bfloat16, jnp.float32
        plane = lax.axis_index("ao")
        occ = lax.axis_index("occ")
        chip, core = occ // 2, occ % 2
        active = (core + plane) % 2 == 1
        place = jnp.stack([plane, chip, core, active.astype(jnp.int32)]).astype(jnp.int32)
        both = ("occ", "ao")
        whole_vmem = pl.BlockSpec(memory_space=pltpu.VMEM)
        whole_smem = pl.BlockSpec(memory_space=pltpu.SMEM)

        def send(x, pairs):
            return lax.ppermute(x, both, pairs)

        def call(body, inputs, outputs, scratch=(), flops=0, moved=0, far_inputs=0, out_space=None, scalars=(), far_space=None):
            near_inputs = len(inputs) - far_inputs
            return pl.pallas_call(
                body,
                out_shape=[jax.ShapeDtypeStruct(s, d) for s, d in outputs],
                in_specs=[whole_smem] * (1 + len(scalars)) + [whole_vmem] * near_inputs + [far_space or hbm] * far_inputs,
                out_specs=out_space or [whole_vmem] * len(outputs),
                scratch_shapes=list(scratch),
                cost_estimate=pl.CostEstimate(flops=flops, bytes_accessed=moved, transcendentals=0),
                compiler_params=pltpu.CompilerParams(vmem_limit_bytes=VMEM_LIMIT),
            )(place, *scalars, *inputs)

        width = 2 if slots % 2 == 0 else 1
        groups, group = slots // width, width * block
        hbm = pl.BlockSpec(memory_space=pl.ANY)
        in_hbm = pl.BlockSpec(memory_space=pltpu.HBM)

        def group_copies(source, to, sems):
            rows = [pl.ds(g * group, group) for g in range(groups)]
            return [pltpu.make_async_copy(source.at[r, :], to.at[r, :], sems.at[g]) for g, r in enumerate(rows)]

        def fit_in_place(metric_ref, ints_ref, copies, turned_ref=None):
            for g, copy in enumerate(copies):
                copy.wait()
                rows = slice(g * group, (g + 1) * group)
                value = jnp.dot(metric_ref[g], ints_ref[rows, :], preferred_element_type=f32).astype(bf16)
                ints_ref[rows, :] = value
                if turned_ref is not None:
                    turned_ref[:, rows] = value.T

        def turn(ints_ref, copies, turned_ref):
            for g, copy in enumerate(copies):
                copy.wait()
                rows = slice(g * group, (g + 1) * group)
                turned_ref[:, rows] = ints_ref[rows, :].T

        def put_halves(at, stage_ref, own_hbm, give_hbm, j, sems, act):
            for h in range(2):
                part = stage_ref.at[j, :, pl.ds(h * half, half)]

                @pl.when(at[2] == h)
                def _():
                    act(pltpu.make_async_copy(part, own_hbm.at[j], sems.at[j, h]))

                @pl.when(at[2] != h)
                def _():
                    act(pltpu.make_async_copy(part, give_hbm.at[j], sems.at[j, h]))

        def start(copy):
            copy.start()

        def wait(copy):
            copy.wait()

        def product(turned_ref, right_ref):
            return jnp.dot(turned_ref[...], right_ref[...], preferred_element_type=f32).astype(bf16)

        raw = half_ints[0]
        far = send(raw, one_core([(0, 3, 1), (1, 0, 2)]))

        piece = (ao_rows, half)
        fitted = (domain, ao_rows)
        product_flops = 2 * domain * ao_rows * ao_rows

        def own_body(
            at, blocks_at, length_at, coef_ref, metric_hbm, raw_hbm,
            metric_ref, turned_ref, keep_ref, give_ref, pair_ref, mine_hbm,
            mine_ref, gathered, sems, metric_sems, mine_sem,
        ):
            rows = [pltpu.make_async_copy(metric_hbm.at[blocks_at[0, s]], gathered.at[s], metric_sems.at[s]) for s in range(slots)]
            for copy in rows:
                copy.start()
            copies = group_copies(raw_hbm, mine_ref, sems)
            for copy in copies:
                copy.start()
            metric_ref[...] = jnp.zeros_like(metric_ref)
            for s, copy in enumerate(rows):
                copy.wait()
                part = slice((s % width) * block, (s % width + 1) * block)
                metric_ref[s // width, part, part] = jnp.where(s < length_at[0], gathered[s], jnp.zeros((), bf16))
            fit_in_place(metric_ref, mine_ref, copies, turned_ref)
            mine_copy = pltpu.make_async_copy(mine_ref, mine_hbm, mine_sem)
            mine_copy.start()
            value = jnp.dot(turned_ref[...], mine_ref[...], preferred_element_type=f32)
            for h in range(2):
                part = value[:, h * half : (h + 1) * half]

                @pl.when(at[2] == h)
                def _():
                    keep_ref[...] = part

                @pl.when(at[2] != h)
                def _():
                    give_ref[...] = part.astype(bf16)

            pair_ref[...] = jnp.dot(coef_ref[...], turned_ref[...], preferred_element_type=f32)
            mine_copy.wait()

        lines = 16
        metric_wide, mine_turned, square_keep, square_give, pair, mine = call(
            own_body,
            [jnp.broadcast_to(coef.T, (lines, ao_rows)), metric_inv, raw],
            [((groups, group, group), bf16), (fitted[::-1], bf16), (piece, f32), (piece, bf16), ((lines, domain), f32), (fitted, bf16)],
            [
                pltpu.VMEM(fitted, bf16),
                pltpu.VMEM((slots, block, block), bf16),
                pltpu.SemaphoreType.DMA((groups,)),
                pltpu.SemaphoreType.DMA((slots,)),
                pltpu.SemaphoreType.DMA,
            ],
            product_flops,
            4 * 2**20,
            far_inputs=2,
            out_space=[whole_vmem] * 5 + [in_hbm],
            scalars=(dom_blocks, dom_len),
            far_space=in_hbm,
        )
        low = send(mine, one_core([(0, 0, 1), (0, 2, 3), (1, 1, 2)]))
        high = send(mine, one_core([(0, 2, 1), (1, 1, 0), (1, 3, 2)]))
        swap = [(i, i ^ 1) for i in range(n_occ)]
        square_got = lax.ppermute(square_give, "occ", swap)
        one_hot = dom_blocks[0][:, None] == jnp.arange(fit_blocks, dtype=jnp.int32)
        density = jnp.einsum(
            "sf,sr->fr",
            one_hot.astype(f32),
            pair[0].reshape(slots, block),
            precision=lax.Precision.HIGHEST,
        )
        for axis, n, bit in (("occ", n_occ, 1), ("occ", n_occ, 2), ("occ", n_occ, 4), ("ao", n_ao, 1), ("ao", n_ao, 2)):
            density = density + lax.ppermute(density, axis, [(i, i ^ bit) for i in range(n)])

        square_tile = (ao_rows, ao_rows)

        def far_body(
            at, metric_ref, turned_ref, far_hbm,
            own_hbm, give_hbm, fit_hbm,
            far_ref, stage, in_sems, out_sems, fit_sem,
        ):
            copies = group_copies(far_hbm, far_ref, in_sems)

            @pl.when((at[3] == 1) & (at[0] >= 1) & (at[0] <= n_ao - 2))
            def _():
                for copy in copies:
                    copy.start()
                fit_in_place(metric_ref, far_ref, copies)
                fit_out = pltpu.make_async_copy(far_ref, fit_hbm, fit_sem)
                fit_out.start()
                stage[0] = product(turned_ref, far_ref)
                put_halves(at, stage, own_hbm, give_hbm, 0, out_sems, start)
                fit_out.wait()
                put_halves(at, stage, own_hbm, give_hbm, 0, out_sems, wait)

        far_own, far_give, far_fit = call(
            far_body,
            [metric_wide, mine_turned, far],
            [((1, *piece), bf16), ((1, *piece), bf16), (fitted, bf16)],
            [
                pltpu.VMEM(fitted, bf16),
                pltpu.VMEM((1, *square_tile), bf16),
                pltpu.SemaphoreType.DMA((groups,)),
                pltpu.SemaphoreType.DMA((1, 2)),
                pltpu.SemaphoreType.DMA,
            ],
            product_flops,
            4 * 2**20,
            far_inputs=1,
            out_space=[in_hbm] * 3,
        )
        far_got = lax.ppermute(far_give, "occ", swap)

        def exchange(pieces):
            parts = [pieces[0]]
            for k in range(1, chips):
                parts.append(lax.ppermute(pieces[k], "occ", [(i, i ^ (2 * k)) for i in range(n_occ)]))
            return parts

        def pick(own_all, got_all, index_of, square_parts=()):
            count = own_all.shape[0]

            def body(at, *refs):
                parts, (own_hbm, got_hbm), rest = refs[: len(square_parts)], refs[len(square_parts) :][:2], refs[len(square_parts) + 2 :]
                outs, sems = rest[:chips], rest[chips]
                busy = at[3] == 1
                steps = []
                for k in range(chips):
                    j = index_of(at[0], at[1] ^ k)
                    safe = jnp.clip(j, 0, count - 1)
                    from_own = pltpu.make_async_copy(own_hbm.at[safe], outs[k], sems.at[k])
                    from_got = pltpu.make_async_copy(got_hbm.at[safe], outs[k], sems.at[k])
                    steps.append((j, from_own, from_got))

                    @pl.when((j >= 0) & busy)
                    def _():
                        from_own.start()

                    @pl.when((j >= 0) & jnp.logical_not(busy))
                    def _():
                        from_got.start()

                for k, (j, from_own, _) in enumerate(steps):
                    if parts:

                        @pl.when(j < 0)
                        def _():
                            outs[k][...] = (parts[0][...] + parts[1][...].astype(f32)).astype(bf16)

                    @pl.when(j >= 0)
                    def _():
                        from_own.wait()

            return call(
                body,
                [*square_parts, own_all, got_all],
                [(piece, bf16)] * chips,
                [pltpu.SemaphoreType.DMA((chips,))],
                0,
                2 * 2**20,
                far_inputs=2,
            )

        def far_index(plane_now, goal):
            return jnp.where(goal == plane_now, -1, 0)

        picked = pick(far_own, far_got, far_index, (square_keep, square_got))
        far_parts = exchange(picked)

        def sum_body(at, a_ref, b_ref, c_ref, d_ref, total_ref, turned_ref, full):
            core_now = at[2]
            full[...] = (
                a_ref[...].astype(f32) + b_ref[...].astype(f32) + c_ref[...].astype(f32) + d_ref[...].astype(f32)
            )
            total_ref[...] = full[...].astype(bf16)
            for h in range(2):
                turned = full[h * half : (h + 1) * half, :].T.astype(bf16)

                @pl.when(core_now == h)
                def _():
                    turned_ref[:half, :] = turned

                @pl.when(core_now != h)
                def _():
                    turned_ref[half:, :] = turned

        def sum_up(parts):
            return call(
                sum_body, parts, [(piece, bf16), ((2 * half, half), bf16)], [pltpu.VMEM(piece, f32)], 0, 2 * 2**20
            )

        def send_turned(turned, moves):
            arrived = send(turned, both_cores(moves))
            return arrived, lax.ppermute(arrived[half:], "occ", swap)

        far_total, far_turned = sum_up(far_parts)

        def near_body(
            at, turned_hbm, low_hbm, high_hbm, fit_hbm,
            own_hbm, give_hbm,
            low_ref, high_ref, far_ref, low_turned, high_turned, turned_ref, stage, in_sems, out_sems, more_sems,
        ):
            plane_now, busy = at[0], at[3] == 1
            has_low, has_high = busy & (plane_now >= 1), busy & (plane_now <= n_ao - 2)
            inner = has_low & has_high
            low_copies = group_copies(low_hbm, low_ref, in_sems.at[0])
            high_copies = group_copies(high_hbm, high_ref, in_sems.at[1])
            turned_copy = pltpu.make_async_copy(turned_hbm, turned_ref, more_sems.at[0])
            far_copy = pltpu.make_async_copy(fit_hbm, far_ref, more_sems.at[1])

            @pl.when(has_low)
            def _():
                for copy in low_copies:
                    copy.start()

            @pl.when(busy)
            def _():
                turned_copy.start()

            @pl.when(has_high)
            def _():
                for copy in high_copies:
                    copy.start()

            @pl.when(inner)
            def _():
                far_copy.start()

            @pl.when(has_low)
            def _():
                turn(low_ref, low_copies, low_turned)

            @pl.when(busy)
            def _():
                turned_copy.wait()

            @pl.when(has_low)
            def _():
                stage[0] = product(turned_ref, low_ref)
                put_halves(at, stage, own_hbm, give_hbm, 0, out_sems, start)

            @pl.when(has_high)
            def _():
                turn(high_ref, high_copies, high_turned)
                stage[1] = product(turned_ref, high_ref)
                put_halves(at, stage, own_hbm, give_hbm, 1, out_sems, start)

            @pl.when(inner)
            def _():
                stage[2] = product(low_turned, high_ref)
                put_halves(at, stage, own_hbm, give_hbm, 2, out_sems, start)
                far_copy.wait()

                @pl.when(plane_now == 1)
                def _():
                    stage[3] = product(low_turned, far_ref)

                @pl.when(plane_now != 1)
                def _():
                    stage[3] = product(high_turned, far_ref)

                put_halves(at, stage, own_hbm, give_hbm, 3, out_sems, start)

            @pl.when(has_low)
            def _():
                put_halves(at, stage, own_hbm, give_hbm, 0, out_sems, wait)

            @pl.when(has_high)
            def _():
                put_halves(at, stage, own_hbm, give_hbm, 1, out_sems, wait)

            @pl.when(inner)
            def _():
                put_halves(at, stage, own_hbm, give_hbm, 2, out_sems, wait)
                put_halves(at, stage, own_hbm, give_hbm, 3, out_sems, wait)

        near_own, near_give = call(
            near_body,
            [mine_turned, low, high, far_fit],
            [((4, *piece), bf16), ((4, *piece), bf16)],
            [
                pltpu.VMEM(fitted, bf16),
                pltpu.VMEM(fitted, bf16),
                pltpu.VMEM(fitted, bf16),
                pltpu.VMEM(fitted[::-1], bf16),
                pltpu.VMEM(fitted[::-1], bf16),
                pltpu.VMEM(fitted[::-1], bf16),
                pltpu.VMEM((4, *square_tile), bf16),
                pltpu.SemaphoreType.DMA((2, groups)),
                pltpu.SemaphoreType.DMA((4, 2)),
                pltpu.SemaphoreType.DMA((2,)),
            ],
            4 * product_flops,
            8 * 2**20,
            far_inputs=4,
            out_space=[in_hbm] * 2,
        )
        near_got = lax.ppermute(near_give, "occ", swap)

        def near_index(plane_now, goal):
            away = goal - plane_now
            beside = jnp.where(away < 0, 0, 1)
            at_end = (plane_now == 0) | (plane_now == n_ao - 1)
            return jnp.where((jnp.abs(away) == 1) | at_end, beside, jnp.where(away == 0, 3, 2))

        picked = pick(near_own, near_got, near_index)
        near_total, near_turned = sum_up(exchange(picked))

        arrived = [
            *send_turned(near_turned, near_turn),
            send(near_total, both_cores(near_straight)),
            *send_turned(far_turned, far_turn),
        ]

        def last_body(at, near_ref, far_ref, ns, no, nd, fs, fo, out_ref):
            plane_now, chip_now, core_now = at[0], at[1], at[2]
            gap = jnp.abs(plane_now - chip_now)
            in_middle = (plane_now >= 1) & (plane_now <= n_ao - 2)
            out_ref[...] = nd[...].astype(f32)

            @pl.when(gap == 1)
            def _():
                out_ref[...] += near_ref[...].astype(f32)

            @pl.when((gap == 0) | ((gap == 2) & in_middle))
            def _():
                out_ref[...] += far_ref[...].astype(f32)

            same_rows = pl.ds(pl.multiple_of(core_now * half, half), half)
            other_rows = pl.ds(pl.multiple_of((1 - core_now) * half, half), half)
            out_ref[same_rows, :] += ns[:half, :].astype(f32) + fs[:half, :].astype(f32)
            out_ref[other_rows, :] += no[...].astype(f32) + fo[...].astype(f32)

        (exchange_k,) = call(last_body, [near_total, far_total, *arrived], [(piece, f32)], [], 0, 3 * 2**20)
        return exchange_k, density.reshape(fit_blocks * block)

    return on_device


def solution(mesh):
    n_occ, n_ao = mesh.shape["occ"], mesh.shape["ao"]
    in_specs = (P("ao", "occ"), P("occ", None, "ao"), P(), P("occ", None), P("occ"))
    out_specs = (P("ao", "occ"), P())

    def sharded(body):
        return jax.shard_map(body, mesh=mesh, in_specs=in_specs, out_specs=out_specs, check_vma=False)

    if not (n_ao == 4 and n_occ == 2 * n_ao):
        return sharded(general_plan)

    def whole(*args):
        if args[1].shape[0] != n_occ:
            return sharded(general_plan)(*args)
        return sharded(line_plan(n_occ, n_ao))(*args)

    return whole
```

```python
import jax
import jax.numpy as jnp
from jax import lax
from jax.experimental import pallas as pl
from jax.experimental.pallas import tpu as pltpu
from jax.sharding import PartitionSpec as P


VMEM_LIMIT = 18 * 2**20


def general_plan(coef, half_ints, metric_inv, dom_blocks, dom_len):
    lmo_count, domain, ao_rows = half_ints.shape
    block = metric_inv.shape[1]
    slots = domain // block
    fit_blocks = metric_inv.shape[0]
    metric_rows = metric_inv[dom_blocks]
    raw_ints = half_ints.reshape(lmo_count, slots, block, ao_rows)
    fitted = jnp.einsum(
        "isab,isbm->isam", metric_rows, raw_ints, preferred_element_type=jnp.float32
    )
    live_slots = jnp.arange(slots, dtype=jnp.int32)[None, :] < dom_len[:, None]
    fitted = jnp.where(live_slots[:, :, None, None], fitted, 0.0)
    fitted = fitted.reshape(lmo_count, domain, ao_rows).astype(jnp.bfloat16)
    pair_part = jnp.einsum("ipm,mi->ip", fitted, coef, preferred_element_type=jnp.float32)
    one_hot = (
        dom_blocks[:, :, None] == jnp.arange(fit_blocks, dtype=jnp.int32)[None, None, :]
    ).astype(jnp.float32)
    local_density = jnp.einsum("isf,isr->fr", one_hot, pair_part.reshape(lmo_count, slots, block))
    density = lax.psum(local_density, ("occ", "ao"))
    density = density.reshape(fit_blocks * block)
    partial_value = jnp.einsum(
        "ipm,ipn->mn",
        fitted,
        lax.all_gather(fitted, "ao", axis=2, tiled=True),
        preferred_element_type=jnp.float32,
    )
    exchange_k = lax.psum_scatter(partial_value, "occ", scatter_dimension=1, tiled=True)
    return (exchange_k, density)


def line_plan(n_occ, n_ao):
    chips = n_occ // 2

    def device(chip, core, plane):
        return (2 * chip + core) * n_ao + plane

    def both_cores(moves):
        return [
            (device(src[1], core, src[0]), device(dst[1], core, dst[0]))
            for src, dst in moves
            for core in range(2)
        ]

    def one_core(moves):
        return [
            (device(chip, core, src), device(chip, core, dst))
            for core, src, dst in moves
            for chip in range(chips)
        ]

    spots = [(p, c) for p in range(n_ao) for c in range(chips)]

    far_turn = [((1, 3), (3, 1)), ((2, 0), (0, 2))]
    copies = {(0, 1): (0, 0), (3, 2): (3, 3)}
    near_turn = [(copies.get((p, c), (p, c)), (c, p)) for p, c in spots if abs(p - c) == 1]
    near_turn += [((1, 3), (2, 0)), ((2, 0), (1, 3)), ((1, 1), (3, 0)), ((2, 2), (0, 3))]
    near_straight = [((1, 3), (0, 2)), ((2, 0), (3, 1)), ((1, 1), (0, 3)), ((2, 2), (3, 0))]

    def on_device(coef, half_ints, metric_inv, dom_blocks, dom_len):
        _, domain, ao_rows = half_ints.shape
        fit_blocks, block, _ = metric_inv.shape
        slots = domain // block
        half = ao_rows // 2
        bf16, f32 = jnp.bfloat16, jnp.float32
        plane = lax.axis_index("ao")
        occ = lax.axis_index("occ")
        chip, core = occ // 2, occ % 2
        active = (core + plane) % 2 == 1
        place = jnp.stack([plane, chip, core, active.astype(jnp.int32)]).astype(jnp.int32)
        both = ("occ", "ao")
        whole_vmem = pl.BlockSpec(memory_space=pltpu.VMEM)
        whole_smem = pl.BlockSpec(memory_space=pltpu.SMEM)

        def send(x, pairs):
            return lax.ppermute(x, both, pairs)

        def call(body, inputs, outputs, scratch=(), flops=0, moved=0, far_inputs=0, out_space=None, scalars=(), far_space=None):
            near_inputs = len(inputs) - far_inputs
            return pl.pallas_call(
                body,
                out_shape=[jax.ShapeDtypeStruct(s, d) for s, d in outputs],
                in_specs=[whole_smem] * (1 + len(scalars)) + [whole_vmem] * near_inputs + [far_space or hbm] * far_inputs,
                out_specs=out_space or [whole_vmem] * len(outputs),
                scratch_shapes=list(scratch),
                cost_estimate=pl.CostEstimate(flops=flops, bytes_accessed=moved, transcendentals=0),
                compiler_params=pltpu.CompilerParams(vmem_limit_bytes=VMEM_LIMIT),
            )(place, *scalars, *inputs)

        width = 2 if slots % 2 == 0 else 1
        groups, group = slots // width, width * block
        hbm = pl.BlockSpec(memory_space=pl.ANY)
        in_hbm = pl.BlockSpec(memory_space=pltpu.HBM)

        def group_copies(source, to, sems):
            rows = [pl.ds(g * group, group) for g in range(groups)]
            return [pltpu.make_async_copy(source.at[r, :], to.at[r, :], sems.at[g]) for g, r in enumerate(rows)]

        def fit_in_place(metric_ref, ints_ref, copies, turned_ref=None):
            for g, copy in enumerate(copies):
                copy.wait()
                rows = slice(g * group, (g + 1) * group)
                value = jnp.dot(metric_ref[g], ints_ref[rows, :], preferred_element_type=f32).astype(bf16)
                ints_ref[rows, :] = value
                if turned_ref is not None:
                    turned_ref[:, rows] = value.T

        def put_halves(at, stage_ref, own_hbm, give_hbm, j, sems, act):
            for h in range(2):
                part = stage_ref.at[j, :, pl.ds(h * half, half)]

                @pl.when(at[2] == h)
                def _():
                    act(pltpu.make_async_copy(part, own_hbm.at[j], sems.at[j, h]))

                @pl.when(at[2] != h)
                def _():
                    act(pltpu.make_async_copy(part, give_hbm.at[j], sems.at[j, h]))

        def start(copy):
            copy.start()

        def wait(copy):
            copy.wait()

        def product(turned_ref, right_ref):
            return jnp.dot(turned_ref[...], right_ref[...], preferred_element_type=f32).astype(bf16)

        raw = half_ints[0]
        far = send(raw, one_core([(0, 3, 1), (1, 0, 2)]))

        piece = (ao_rows, half)
        fitted = (domain, ao_rows)
        depth = domain // 2
        product_flops = 2 * domain * ao_rows * ao_rows

        def own_body(
            at, blocks_at, length_at, coef_ref, metric_hbm, raw_hbm,
            metric_ref, turned_ref, keep_ref, give_ref, pair_ref, first_hbm, second_hbm,
            mine_ref, gathered, sems, metric_sems, mine_sems,
        ):
            rows = [pltpu.make_async_copy(metric_hbm.at[blocks_at[0, s]], gathered.at[s], metric_sems.at[s]) for s in range(slots)]
            for copy in rows:
                copy.start()
            copies = group_copies(raw_hbm, mine_ref, sems)
            for copy in copies:
                copy.start()
            metric_ref[...] = jnp.zeros_like(metric_ref)
            for s, copy in enumerate(rows):
                copy.wait()
                part = slice((s % width) * block, (s % width + 1) * block)
                metric_ref[s // width, part, part] = jnp.where(s < length_at[0], gathered[s], jnp.zeros((), bf16))
            fit_in_place(metric_ref, mine_ref, copies, turned_ref)
            outs = [
                pltpu.make_async_copy(mine_ref.at[pl.ds(i * depth, depth), :], out, mine_sems.at[i])
                for i, out in enumerate((first_hbm, second_hbm))
            ]
            for copy in outs:
                copy.start()
            value = jnp.dot(turned_ref[...], mine_ref[...], preferred_element_type=f32)
            for h in range(2):
                part = value[:, h * half : (h + 1) * half]

                @pl.when(at[2] == h)
                def _():
                    keep_ref[...] = part

                @pl.when(at[2] != h)
                def _():
                    give_ref[...] = part.astype(bf16)

            pair_ref[...] = jnp.dot(coef_ref[...], turned_ref[...], preferred_element_type=f32)
            for copy in outs:
                copy.wait()

        lines = 16
        metric_wide, mine_turned, square_keep, square_give, pair, *mine = call(
            own_body,
            [jnp.broadcast_to(coef.T, (lines, ao_rows)), *(pltpu.with_memory_space_constraint(x, pltpu.HBM) for x in (metric_inv, raw))],
            [((groups, group, group), bf16), (fitted[::-1], bf16), (piece, f32), (piece, bf16), ((lines, domain), f32), *[((depth, ao_rows), bf16)] * 2],
            [
                pltpu.VMEM(fitted, bf16),
                pltpu.VMEM((slots, block, block), bf16),
                pltpu.SemaphoreType.DMA((groups,)),
                pltpu.SemaphoreType.DMA((slots,)),
                pltpu.SemaphoreType.DMA((2,)),
            ],
            product_flops,
            4 * 2**20,
            far_inputs=2,
            out_space=[whole_vmem] * 5 + [in_hbm] * 2,
            scalars=(dom_blocks, dom_len),
            far_space=in_hbm,
        )
        low_moves = one_core([(0, 0, 1), (0, 2, 3), (1, 1, 2)])
        high_moves = one_core([(0, 2, 1), (1, 1, 0), (1, 3, 2)])
        low = [send(part, low_moves) for part in mine]
        high = [send(part, high_moves) for part in mine]
        swap = [(i, i ^ 1) for i in range(n_occ)]
        square_got = lax.ppermute(square_give, "occ", swap)
        one_hot = dom_blocks[0][:, None] == jnp.arange(fit_blocks, dtype=jnp.int32)
        density = jnp.einsum(
            "sf,sr->fr",
            one_hot.astype(f32),
            pair[0].reshape(slots, block),
            precision=lax.Precision.HIGHEST,
        )
        for axis, n, bit in (("occ", n_occ, 1), ("occ", n_occ, 2), ("occ", n_occ, 4), ("ao", n_ao, 1), ("ao", n_ao, 2)):
            density = density + lax.ppermute(density, axis, [(i, i ^ bit) for i in range(n)])

        square_tile = (ao_rows, ao_rows)

        def far_body(
            at, metric_ref, turned_ref, far_hbm,
            own_hbm, give_hbm, fit_hbm,
            far_ref, stage, in_sems, out_sems, fit_sem,
        ):
            copies = group_copies(far_hbm, far_ref, in_sems)

            @pl.when((at[3] == 1) & (at[0] >= 1) & (at[0] <= n_ao - 2))
            def _():
                for copy in copies:
                    copy.start()
                fit_in_place(metric_ref, far_ref, copies)
                fit_out = pltpu.make_async_copy(far_ref, fit_hbm, fit_sem)
                fit_out.start()
                stage[0] = product(turned_ref, far_ref)
                put_halves(at, stage, own_hbm, give_hbm, 0, out_sems, start)
                fit_out.wait()
                put_halves(at, stage, own_hbm, give_hbm, 0, out_sems, wait)

        far_own, far_give, far_fit = call(
            far_body,
            [metric_wide, mine_turned, far],
            [((1, *piece), bf16), ((1, *piece), bf16), (fitted, bf16)],
            [
                pltpu.VMEM(fitted, bf16),
                pltpu.VMEM((1, *square_tile), bf16),
                pltpu.SemaphoreType.DMA((groups,)),
                pltpu.SemaphoreType.DMA((1, 2)),
                pltpu.SemaphoreType.DMA,
            ],
            product_flops,
            4 * 2**20,
            far_inputs=1,
            out_space=[in_hbm] * 3,
        )
        far_got = lax.ppermute(far_give, "occ", swap)

        def exchange(pieces):
            parts = [pieces[0]]
            for k in range(1, chips):
                parts.append(lax.ppermute(pieces[k], "occ", [(i, i ^ (2 * k)) for i in range(n_occ)]))
            return parts

        def pick(own_all, got_all, index_of, square_parts=()):
            count = own_all.shape[0]

            def body(at, *refs):
                parts, (own_hbm, got_hbm), rest = refs[: len(square_parts)], refs[len(square_parts) :][:2], refs[len(square_parts) + 2 :]
                outs, sems = rest[:chips], rest[chips]
                busy = at[3] == 1
                steps = []
                for k in range(chips):
                    j = index_of(at[0], at[1] ^ k)
                    safe = jnp.clip(j, 0, count - 1)
                    from_own = pltpu.make_async_copy(own_hbm.at[safe], outs[k], sems.at[k])
                    from_got = pltpu.make_async_copy(got_hbm.at[safe], outs[k], sems.at[k])
                    steps.append((j, from_own, from_got))

                    @pl.when((j >= 0) & busy)
                    def _():
                        from_own.start()

                    @pl.when((j >= 0) & jnp.logical_not(busy))
                    def _():
                        from_got.start()

                for k, (j, from_own, _) in enumerate(steps):
                    if parts:

                        @pl.when(j < 0)
                        def _():
                            outs[k][...] = (parts[0][...] + parts[1][...].astype(f32)).astype(bf16)

                    @pl.when(j >= 0)
                    def _():
                        from_own.wait()

            return call(
                body,
                [*square_parts, own_all, got_all],
                [(piece, bf16)] * chips,
                [pltpu.SemaphoreType.DMA((chips,))],
                0,
                2 * 2**20,
                far_inputs=2,
            )

        def far_index(plane_now, goal):
            return jnp.where(goal == plane_now, -1, 0)

        picked = pick(far_own, far_got, far_index, (square_keep, square_got))
        far_parts = exchange(picked)

        def sum_body(at, a_ref, b_ref, c_ref, d_ref, total_ref, turned_ref, full):
            core_now = at[2]
            full[...] = (
                a_ref[...].astype(f32) + b_ref[...].astype(f32) + c_ref[...].astype(f32) + d_ref[...].astype(f32)
            )
            total_ref[...] = full[...].astype(bf16)
            for h in range(2):
                turned = full[h * half : (h + 1) * half, :].T.astype(bf16)

                @pl.when(core_now == h)
                def _():
                    turned_ref[:half, :] = turned

                @pl.when(core_now != h)
                def _():
                    turned_ref[half:, :] = turned

        def sum_up(parts):
            return call(
                sum_body, parts, [(piece, bf16), ((2 * half, half), bf16)], [pltpu.VMEM(piece, f32)], 0, 2 * 2**20
            )

        def send_turned(turned, moves):
            arrived = send(turned, both_cores(moves))
            return arrived, lax.ppermute(arrived[half:], "occ", swap)

        far_total, far_turned = sum_up(far_parts)

        def near_products(part, low_part, high_part, before=()):
            is_last = bool(before)

            def body(at, *refs):
                acc_in, refs = (refs[0], refs[1:]) if is_last else (None, refs)
                turned_hbm, low_hbm, high_hbm, fit_hbm, *refs = refs
                outs, refs = (refs[:2], refs[2:]) if is_last else (refs[:1], refs[1:])
                low_ref, high_ref, far_ref, outer_ref, turned_ref, sems, *rest = refs
                plane_now, busy = at[0], at[3] == 1
                has_low, has_high = busy & (plane_now >= 1), busy & (plane_now <= n_ao - 2)
                inner = has_low & has_high
                span = pl.ds(part * depth, depth)
                low_copy = pltpu.make_async_copy(low_hbm, low_ref, sems.at[0])
                high_copy = pltpu.make_async_copy(high_hbm, high_ref, sems.at[1])
                turned_copy = pltpu.make_async_copy(turned_hbm.at[:, span], turned_ref, sems.at[2])
                far_copy = pltpu.make_async_copy(fit_hbm.at[span, :], far_ref, sems.at[3])

                def put(j, left_ref, right_ref):
                    value = jnp.dot(left_ref[...], right_ref[...], preferred_element_type=f32)
                    if is_last:
                        rest[0][j] = (acc_in[j] + value).astype(bf16)
                        put_halves(at, rest[0], *outs, j, rest[1], start)
                    else:
                        outs[0][j] = value

                @pl.when(has_low)
                def _():
                    low_copy.start()

                @pl.when(busy)
                def _():
                    turned_copy.start()

                @pl.when(has_high)
                def _():
                    high_copy.start()

                @pl.when(inner)
                def _():
                    far_copy.start()

                @pl.when(busy)
                def _():
                    turned_copy.wait()

                @pl.when(has_low)
                def _():
                    low_copy.wait()
                    put(0, turned_ref, low_ref)

                @pl.when(has_high)
                def _():
                    high_copy.wait()
                    put(1, turned_ref, high_ref)

                @pl.when(inner & (plane_now == 1))
                def _():
                    outer_ref[...] = low_ref[...].T
                    put(2, outer_ref, high_ref)

                @pl.when(inner & (plane_now != 1))
                def _():
                    outer_ref[...] = high_ref[...].T
                    put(2, outer_ref, low_ref)

                @pl.when(inner)
                def _():
                    far_copy.wait()
                    put(3, outer_ref, far_ref)

                if is_last:

                    @pl.when(has_low)
                    def _():
                        put_halves(at, rest[0], *outs, 0, rest[1], wait)

                    @pl.when(has_high)
                    def _():
                        put_halves(at, rest[0], *outs, 1, rest[1], wait)

                    @pl.when(inner)
                    def _():
                        put_halves(at, rest[0], *outs, 2, rest[1], wait)
                        put_halves(at, rest[0], *outs, 3, rest[1], wait)

            shard = pltpu.VMEM((depth, ao_rows), bf16)
            last_scratch = [pltpu.VMEM((4, *square_tile), bf16), pltpu.SemaphoreType.DMA((4, 2))]
            return call(
                body,
                [*before, mine_turned, low_part, high_part, far_fit],
                [((4, *piece), bf16)] * 2 if is_last else [((4, *square_tile), f32)],
                [
                    shard,
                    shard,
                    shard,
                    pltpu.VMEM((ao_rows, depth), bf16),
                    pltpu.VMEM((ao_rows, depth), bf16),
                    pltpu.SemaphoreType.DMA((4,)),
                    *(last_scratch if is_last else []),
                ],
                2 * product_flops,
                6 * 2**20,
                far_inputs=4,
                out_space=[in_hbm] * 2 if is_last else [whole_vmem],
            )

        before = near_products(0, low[0], high[0])
        near_own, near_give = near_products(1, low[1], high[1], before)
        near_got = lax.ppermute(near_give, "occ", swap)

        def near_index(plane_now, goal):
            away = goal - plane_now
            beside = jnp.where((away < 0) | (plane_now == n_ao - 1), 0, 1)
            at_end = (plane_now == 0) | (plane_now == n_ao - 1)
            return jnp.where((jnp.abs(away) == 1) | at_end, beside, jnp.where(away == 0, 3, 2))

        picked = pick(near_own, near_got, near_index)
        near_total, near_turned = sum_up(exchange(picked))

        arrived = [
            *send_turned(near_turned, near_turn),
            send(near_total, both_cores(near_straight)),
            *send_turned(far_turned, far_turn),
        ]

        def last_body(at, near_ref, far_ref, ns, no, nd, fs, fo, out_ref):
            plane_now, chip_now, core_now = at[0], at[1], at[2]
            gap = jnp.abs(plane_now - chip_now)
            in_middle = (plane_now >= 1) & (plane_now <= n_ao - 2)
            from_far = (gap == 0) | ((gap == 2) & in_middle)
            for h in range(2):
                rows = slice(h * half, (h + 1) * half)
                own_half = core_now == h
                base = jnp.where(gap == 1, near_ref[rows, :], far_ref[rows, :]).astype(f32)
                base = jnp.where((gap == 1) | from_far, base, 0.0)
                turned = jnp.where(own_half, ns[:half, :], no[...]).astype(f32)
                turned += jnp.where(own_half, fs[:half, :], fo[...]).astype(f32)
                out_ref[rows, :] = nd[rows, :].astype(f32) + base + turned

        (exchange_k,) = call(last_body, [near_total, far_total, *arrived], [(piece, f32)], [], 0, 3 * 2**20)
        return exchange_k, density.reshape(fit_blocks * block)

    return on_device


def solution(mesh):
    n_occ, n_ao = mesh.shape["occ"], mesh.shape["ao"]
    in_specs = (P("ao", "occ"), P("occ", None, "ao"), P(), P("occ", None), P("occ"))
    out_specs = (P("ao", "occ"), P())

    def sharded(body):
        return jax.shard_map(body, mesh=mesh, in_specs=in_specs, out_specs=out_specs, check_vma=False)

    if not (n_ao == 4 and n_occ == 2 * n_ao):
        return sharded(general_plan)

    def whole(*args):
        if args[1].shape[0] != n_occ:
            return sharded(general_plan)(*args)
        return sharded(line_plan(n_occ, n_ao))(*args)

    return whole
```
